768 devices in a mesh: region: 768 (over x, z, y, core).
Axes of the slice: x: 4, y: 8, z: 12, core: 2. Of those that a mesh axis runs over, the one named last changes fastest.
Arguments:
- coefficients: float32 [9, 35, 98304], P(None, None, 'region'), may hold values from -6 to 6
- star_matrices: float32 [3, 9, 9, 98304], P(None, None, None, 'region'), may hold values from -4.4 to 4.4
- flux_solvers: float32 [2, 4, 9, 9, 98304], P(None, None, None, None, 'region'), may hold values from -2 to 2
- stiffness: float32 [3, 35, 35], replicated, may hold values from -1 to 1
- projection: float32 [4, 15, 35], replicated, may hold values from -1 to 1
- lifting: float32 [4, 35, 15], replicated, may hold values from -1 to 1
- block_cluster: int32 [6144], P('region'), may hold values from 0 to 2, as said below
- neighbors: int32 [4, 98304], P(None, 'region'), may hold values from 0 to 767, as said below
- send_faces: int32 [4, 49152], P(None, 'region'), may hold values from 0 to 511, as said below
Outputs:
- updated: float32 [9, 35, 98304], P(None, None, 'region')
The draws below stay inside these ranges and needn't reach their ends.
Inputs may be any that keep to these rules, and one draw needn't show every extreme that they name: `block_cluster`: the cluster of each block of 16 consecutive elements of a device, blocks in the device's order. `neighbors`: entry [f, e] of a device is a column of that device's face table: f2 * 128 + e2 for a face f2 of an element e2 of the same device (the face itself for faces on the outer surface and for faces listed toward a device beyond the ends of the curve), or 512 + k * 64 + j for the face in slot j of the device's list k, when the device r + o(k), o = (-1, -2, 2, 1), exists. Faces paired within a device name each other. `send_faces`: list k of a device holds 64 distinct faces f * 128 + e of that device, no face in two lists; slot j of list k of device r meets slot j of list 3 - k of device r + o(k), o = (-1, -2, 2, 1).
All inputs are finite; a program needn't handle non-finite values.
Results may differ from the reference program's by a relative error of at most 0.0003.
Values sent between devices are 32-bit elements; how exact they have to be, the bound alone decides.
No kernel may reach another device: no remote copies, remote signals or barrier semaphores. Data moves between devices by JAX's collectives and lax.ppermute only.
A program may use at most 64 MiB of HBM per device.

```python
import jax
import jax.numpy as jnp
from jax import lax

NQ = 9
BASIS = 35
FACE_BASIS = 15
DERIVS = 5
TICKS = 4
BLOCK = 16
NBLK = 8
ELEM_DEV = 128
SLOT = 64
NDEV = 768
TOTAL_E = 98304


def face_layout(key):
    base_key = jax.random.fold_in(key, 7)
    faces = 4 * ELEM_DEV
    remote = 4 * SLOT
    offsets = jnp.array([-1, -2, 2, 1], dtype=jnp.int32)

    def one_device(device):
        device_key = jax.random.fold_in(base_key, device)
        key_order, key_outer = jax.random.split(device_key)
        ordering = jax.random.permutation(key_order, faces).astype(jnp.int32)
        position = jnp.arange(faces, dtype=jnp.int32)
        last_face = faces - 1
        forced = jnp.where(ordering == last_face, ordering[0], jnp.where(position == 0, last_face, ordering))
        ordering = jnp.where(device == 0, forced, ordering)
        group = jnp.minimum(position // SLOT, 3)
        target = device + offsets[group]
        present = (target >= 0) & (target < NDEV)
        outer = jax.random.randint(key_outer, (faces // 2,), 0, 4) == 0
        partner = ordering[jnp.bitwise_xor(position, 1)]
        local_value = jnp.where(outer[position // 2], ordering, partner)
        value = jnp.where(position < remote, jnp.where(present, faces + position, ordering), local_value)
        lookup = jnp.zeros((faces,), jnp.int32).at[ordering].set(value.astype(jnp.int32))
        return (lookup.reshape(4, ELEM_DEV), ordering[:remote].reshape(4, SLOT))
    lookups, listed = jax.vmap(one_device)(jnp.arange(NDEV, dtype=jnp.int32))
    return (lookups, listed)


def draw_neighbors(key, part):
    lookups, listed = face_layout(key)
    return jnp.transpose(lookups, (1, 0, 2)).reshape(4, NDEV * ELEM_DEV).astype(jnp.int32)


def draw_send_faces(key, part):
    lookups, listed = face_layout(key)
    return jnp.transpose(listed, (1, 0, 2)).reshape(4, NDEV * SLOT).astype(jnp.int32)


def cluster_layout(key):
    base_key = jax.random.fold_in(key, 11)
    key_centre, key_roll = jax.random.split(base_key)
    centre = jax.random.randint(key_centre, (), 0, NDEV)
    span = max(NDEV // 8, 1)
    device = jnp.arange(NDEV * NBLK, dtype=jnp.int32) // NBLK
    inside = jnp.abs(device - centre) * 2 < span
    rolled = jax.random.randint(key_roll, (NDEV * NBLK,), 0, 8)
    cluster = jnp.where(rolled == 0, 0, jnp.where(rolled < 4, 1, 2))
    cluster = jnp.where(inside, 0, cluster)
    cluster = cluster.at[NDEV * NBLK - 1].set(2)
    return cluster.astype(jnp.int32)


def draw_block_cluster(key, part):
    return cluster_layout(key)


def draw_star_matrices(key, part):
    cluster = cluster_layout(key)
    element_cluster = jnp.repeat(cluster, BLOCK)
    period = jnp.where(element_cluster == 0, 1.0, jnp.where(element_cluster == 1, 2.0, 4.0)).astype(jnp.float32)
    star_key = jax.random.fold_in(key, 13)
    entries = jax.random.truncated_normal(star_key, -4.0, 4.0, (3, NQ, NQ, NDEV * ELEM_DEV), jnp.float32)
    return (entries * (1.1 / period)[None, None, None, :]).astype(jnp.float32)


def block_levels(stream_key, dims, shards, low, largest):
    gain = 1.0
    for dim, parts in shards:
        heights = jax.random.uniform(jax.random.fold_in(jax.random.fold_in(stream_key, 6), dim), (parts,), jnp.float32, low / len(shards), largest / len(shards))
        gain = gain * jnp.repeat(jnp.exp(heights), dims[dim] // parts).reshape((-1,) + (1,) * (len(dims) - 1 - dim))
    return gain


def gaussian(own_key, shape, deviation, bound, shards=(), kind=jnp.bfloat16):
    result = deviation * jax.random.normal(own_key, shape, jnp.float32)
    if shards:
        result = result * block_levels(own_key, shape, shards, -0.22, 0.18)
    return jnp.clip(result, -bound, bound).astype(kind)


def setup_inputs(seed: int = 0) -> dict:
    key_of = jax.random.split(jax.random.key(seed), 10)
    coefficients = gaussian(key_of[0], (NQ, BASIS, TOTAL_E), 1.0, 6.0, ((2, 768),), jnp.float32)
    star_matrices = draw_star_matrices(jax.random.fold_in(key_of[9], 71), 0)
    flux_solvers = gaussian(key_of[2], (2, 4, NQ, NQ, TOTAL_E), NQ ** -0.5, 2.0, ((4, 768),), jnp.float32)
    stiffness = gaussian(key_of[3], (3, BASIS, BASIS), BASIS ** -0.5, 1.0, (), jnp.float32)
    projection = gaussian(key_of[4], (4, FACE_BASIS, BASIS), BASIS ** -0.5, 1.0, (), jnp.float32)
    lifting = gaussian(key_of[5], (4, BASIS, FACE_BASIS), (2 * FACE_BASIS) ** -0.5, 1.0, (), jnp.float32)
    block_cluster = draw_block_cluster(jax.random.fold_in(key_of[9], 71), 0)
    neighbors = draw_neighbors(jax.random.fold_in(key_of[9], 71), 0)
    send_faces = draw_send_faces(jax.random.fold_in(key_of[9], 71), 0)
    return {"coefficients": coefficients, "star_matrices": star_matrices, "flux_solvers": flux_solvers, "stiffness": stiffness, "projection": projection, "lifting": lifting, "block_cluster": block_cluster, "neighbors": neighbors, "send_faces": send_faces}


quarter_step = 0.125
factorials = (1.0, 1.0, 2.0, 6.0, 24.0, 120.0)
curve_offsets = (-1, -2, 2, 1)
highest = lax.Precision.HIGHEST


def predict(values, matrices, stiffness):
    derivatives = [values]
    current = values
    for degree in range(DERIVS - 1):
        stiffened = jnp.einsum('dab,qbe->dqae', stiffness, current, precision=highest)
        current = -jnp.einsum('dqae,dqpe->pae', stiffened, matrices, precision=highest)
        derivatives.append(current)
    return derivatives


def integrate(derivatives, begin_time, finish):
    integral = jnp.zeros_like(derivatives[0])
    for degree in range(len(derivatives)):
        weight = (finish ** (degree + 1) - begin_time ** (degree + 1)) / factorials[degree + 1]
        integral = integral + weight * derivatives[degree]
    return integral


def update(values, own_part, near_part, matrices, solvers, stiffness, projection, lifting):
    own_faces = jnp.einsum('fib,qbe->qife', projection, own_part, precision=highest)
    face_flux = jnp.einsum('qife,fqpe->pife', own_faces, solvers[0], precision=highest) + jnp.einsum('qife,fqpe->pife', near_part, solvers[1], precision=highest)
    surface = jnp.einsum('fai,pife->pae', lifting, face_flux, precision=highest)
    stiffened = jnp.einsum('dba,qbe->dqae', stiffness, own_part, precision=highest)
    volume = jnp.einsum('dqae,dqpe->pae', stiffened, matrices, precision=highest)
    return values + volume - surface


def by_device(array):
    shaped = array.reshape(array.shape[:-1] + (NDEV, ELEM_DEV))
    return jnp.moveaxis(shaped, -2, 0)


def pick_columns(source_table, column_ids):
    return jnp.take(source_table, column_ids, axis=1)


def reference(coefficients, star_matrices, flux_solvers, stiffness, projection, lifting, block_cluster, neighbors, send_faces):
    quantities, basis_size, element_total = coefficients.shape
    face_rows = quantities * FACE_BASIS
    current_state = by_device(coefficients)
    star_parts = by_device(star_matrices)
    flux_parts = by_device(flux_solvers)
    cluster_parts = jnp.repeat(block_cluster, BLOCK).reshape(NDEV, ELEM_DEV)
    period_parts = jnp.where(cluster_parts == 0, 1, jnp.where(cluster_parts == 1, 2, 4)).astype(jnp.int32)
    neighbor_parts = by_device(neighbors).reshape(NDEV, 4 * ELEM_DEV)
    send_parts = jnp.moveaxis(send_faces.reshape(4, NDEV, SLOT), 1, 0)
    neighbor_sum = jnp.zeros((NDEV, face_rows, 4 * ELEM_DEV), jnp.float32)
    for tick_index in range(TICKS):
        def local_pass(items):
            values, matrices, period = items
            derivatives = predict(values, matrices, stiffness)
            begin_time = (tick_index % period).astype(jnp.float32) * quarter_step
            tick_integral = integrate(derivatives, begin_time, begin_time + quarter_step)
            own_integral = integrate(derivatives, 0.0, period.astype(jnp.float32) * quarter_step)
            face_data = jnp.einsum('fib,qbe->qife', projection, tick_integral, precision=highest)
            return face_data.reshape(face_rows, 4 * ELEM_DEV), own_integral

        local_faces, own_parts = lax.map(local_pass, (current_state, star_parts, period_parts))
        outgoing = jax.vmap(pick_columns)(local_faces, send_parts)
        arrived = []
        for column, offset in enumerate(curve_offsets):
            padded = jnp.pad(outgoing[:, :, 3 - column, :], ((2, 2), (0, 0), (0, 0)))
            arrived.append(padded[2 + offset:2 + offset + NDEV])
        received = jnp.stack(arrived, axis=2).reshape(NDEV, face_rows, 4 * SLOT)
        face_table = jnp.concatenate([local_faces, received], axis=2)
        neighbor_sum = neighbor_sum + jax.vmap(pick_columns)(face_table, neighbor_parts)

        def finish_pass(items):
            values, own_part, near_part, matrices, solvers, period = items
            ending = (tick_index + 1) % period == 0
            near_faces = near_part.reshape(quantities, FACE_BASIS, 4, ELEM_DEV)
            advanced = update(values, own_part, near_faces, matrices, solvers, stiffness, projection, lifting)
            values = jnp.where(ending[None, None, :], advanced, values)
            cleared = jnp.where(ending[None, None, :], 0.0, near_part.reshape(face_rows, 4, ELEM_DEV))
            return values, cleared.reshape(face_rows, 4 * ELEM_DEV)

        current_state, neighbor_sum = lax.map(finish_pass, (current_state, own_parts, neighbor_sum, star_parts, flux_parts, period_parts))
    return jnp.moveaxis(current_state, 0, -2).reshape(quantities, basis_size, element_total)
```

```python
import functools

import jax
import jax.numpy as jnp
from jax import lax
from jax.experimental import pallas as pl
from jax.experimental.pallas import tpu as pltpu
from jax.sharding import PartitionSpec as P

NQ = 9
BASIS = 35
ROWS = 40
FACES = 4
FACE_BASIS = 15
FACE_ROWS = 16
DERIVS = 5
TICKS = 4
LANES = 128
BLOCK = 16
STEP = 0.125
FACTORIALS = (1.0, 2.0, 6.0, 24.0, 120.0)
F32 = jnp.float32
BF16 = jnp.bfloat16
TABLE = NQ * FACE_ROWS
WIDE = NQ * LANES


def split_pair(x):
    high = x.astype(BF16)
    return high, (x - high.astype(F32)).astype(BF16)


def stacked(x, depth):
    high = x.astype(BF16).astype(F32)
    parts = [high, x - high, high]
    rest = depth - 3 * x.shape[0]
    if rest:
        parts.append(jnp.zeros((rest, x.shape[1]), F32))
    return jnp.concatenate(parts, axis=0).astype(BF16)


def placed(block, offset, width, rows):
    source = lax.broadcasted_iota(jnp.int32, (block.shape[1], width), 0)
    target = lax.broadcasted_iota(jnp.int32, (block.shape[1], width), 1)
    chosen = (target == source + offset).astype(BF16)
    return jnp.dot(block, chosen, preferred_element_type=F32)


def weights_into(ref, row, block, stride):
    high, low = split_pair(block)
    width = ref.shape[1]
    full = (
        placed(high, 0, width, 0) + placed(high, stride, width, 0) + placed(low, 2 * stride, width, 0)
    )
    ref[row : row + block.shape[0], :] = full


def wide(ref):
    return jnp.concatenate([ref[q] for q in range(NQ)], axis=1)


def matmul(weights, x):
    return jnp.dot(weights, x, preferred_element_type=F32)


def contract_star(blocks, base, star_ref, finish):
    for first in range(0, NQ, 3):
        totals = [None] * 3
        for direction in range(3):
            for source in range(NQ):
                block = blocks[
                    base + direction * ROWS : base + (direction + 1) * ROWS,
                    source * LANES : (source + 1) * LANES,
                ]
                for k in range(3):
                    term = block * star_ref[direction, source, first + k : first + k + 1, :]
                    totals[k] = term if totals[k] is None else totals[k] + term
        for k in range(3):
            finish(first + k, totals[k])


def tick_weights(period, tick):
    out = []
    for k in range(DERIVS):
        values = []
        for p in (1, 2, 4):
            s = STEP * (tick % p)
            values.append(((s + STEP) ** (k + 1) - s ** (k + 1)) / FACTORIALS[k])
        out.append(jnp.where(period == 1, values[0], jnp.where(period == 2, values[1], values[2])))
    return out


def own_weights(period):
    out = []
    for k in range(DERIVS):
        values = [(STEP * p) ** (k + 1) / FACTORIALS[k] for p in (1, 2, 4)]
        out.append(jnp.where(period == 1, values[0], jnp.where(period == 2, values[1], values[2])))
    return out


def predict_and_send(
    tick, first_state, star_ref, stiff_ref, proj_ref, send_ref, period_ref,
    table_ref, own_ref, near_list_ref, far_list_ref, derivs, blocks, faces,
):
    def degree(k, carry):
        x = jnp.concatenate([derivs[k, q] for q in range(NQ)], axis=1)
        blocks[...] = matmul(stiff_ref[...], stacked(x, LANES))

        def finish(p, total):
            derivs[k + 1, p] = total

        contract_star(blocks, 0, star_ref, finish)
        return carry

    lax.fori_loop(0, DERIVS - 1, degree, 0)
    period = period_ref[0:1, :]
    now = tick_weights(period, tick)
    whole = own_weights(period)
    parts = []
    for q in range(NQ):
        tick_sum = None
        own_sum = None
        for k in range(DERIVS):
            d = derivs[k, q]
            a, b = d * now[k], d * whole[k]
            tick_sum = a if tick_sum is None else tick_sum + a
            own_sum = b if own_sum is None else own_sum + b
        own_ref[q] = own_sum
        parts.append(tick_sum)
    faces[...] = matmul(proj_ref[...], stacked(jnp.concatenate(parts, axis=1), LANES))
    highs, lows = [], []
    for q in range(NQ):
        row = jnp.concatenate(
            [
                faces[f * FACE_ROWS : (f + 1) * FACE_ROWS, q * LANES : (q + 1) * LANES]
                for f in range(FACES)
            ],
            axis=1,
        )
        high, low = split_pair(row)
        table_ref[q * FACE_ROWS : (q + 1) * FACE_ROWS, :] = high
        table_ref[TABLE + q * FACE_ROWS : TABLE + (q + 1) * FACE_ROWS, :] = low
    both = matmul(table_ref[...], send_ref[...])
    picked = both[:TABLE] + both[TABLE:]
    near_list_ref[...] = picked[:, :LANES]
    far_list_ref[...] = picked[:, LANES:]


def begin_kernel(
    coef_ref, star_ref, stiffness_ref, projection_ref, cluster_ref, faces_ref,
    state_ref, own_ref, table_ref, near_list_ref, far_list_ref,
    stiff_ref, proj_ref, send_ref, period_ref,
    derivs, blocks, faces, work,
):
    lane = lax.broadcasted_iota(jnp.int32, (8, LANES), 1)
    period = jnp.full((8, LANES), 1, jnp.int32)
    for j in range(LANES // BLOCK):
        c = cluster_ref[j]
        p = jnp.where(c == 0, 1, jnp.where(c == 1, 2, 4))
        period = jnp.where(lane // BLOCK == j, p, period)
    period_ref[...] = period
    derivs[0] = jnp.zeros((NQ, ROWS, LANES), F32)
    for q in range(NQ):
        derivs[0, q, 0:BASIS, :] = coef_ref[q]
    state_ref[...] = derivs[0]
    work[...] = jnp.zeros_like(work)
    for d in range(3):
        weights_into(work, d * ROWS, -stiffness_ref[d], ROWS)
    stiff_ref[...] = work[0 : 3 * ROWS, :].astype(BF16)
    work[...] = jnp.zeros_like(work)
    for f in range(FACES):
        weights_into(work, f * FACE_ROWS, projection_ref[f], ROWS)
    proj_ref[...] = work[0 : FACES * FACE_ROWS, :].astype(BF16)
    column = lax.broadcasted_iota(jnp.int32, (FACES * LANES, LANES), 0)
    near = jnp.concatenate([faces_ref[3:4, :], faces_ref[0:1, :]], axis=1)
    far = jnp.concatenate([faces_ref[1:2, :], faces_ref[2:3, :]], axis=1)
    send_ref[:, :LANES] = (column == near).astype(F32).astype(BF16)
    send_ref[:, LANES:] = (column == far).astype(F32).astype(BF16)
    predict_and_send(
        0, None, star_ref, stiff_ref, proj_ref, send_ref, period_ref,
        table_ref, own_ref, near_list_ref, far_list_ref, derivs, blocks, faces,
    )


def relay_kernel(gathered_ref, far_list_ref, first_ref, second_ref):
    me = lax.axis_index("region")
    other = 1 - lax.rem(me, 2)
    even = lax.rem(me // 2, 2) == 0
    lane = lax.broadcasted_iota(jnp.int32, (TABLE, LANES), 1)
    partner = gathered_ref[other]
    own = far_list_ref[...]
    upward = jnp.where(lane < LANES // 2, partner, own)
    downward = jnp.where(lane < LANES // 2, own, partner)
    first_ref[...] = jnp.where(even, downward, upward)
    second_ref[...] = jnp.where(even, upward, downward)


def face_contract(source, solver_ref, side, into):
    for f in range(FACES):
        totals = [None] * NQ
        for q in range(NQ):
            block = source(q, f)
            for p in range(NQ):
                term = block * solver_ref[side, f, q, p : p + 1, :]
                totals[p] = term if totals[p] is None else totals[p] + term
        for p in range(NQ):
            into[f * FACE_ROWS : (f + 1) * FACE_ROWS, p * LANES : (p + 1) * LANES] = totals[p]


def ending_mask(period, tick):
    return lax.rem(jnp.full_like(period, tick + 1), period) == 0


def own_body(
    tick, state_ref, own_ref, table_ref, sum_ref, star_ref, solver_ref, period_ref,
    both_ref, lift_ref, local_ref, base_ref, partial_ref, big, flux,
):
    ending = ending_mask(period_ref[0:1, :], tick)
    big[...] = matmul(both_ref[...], stacked(wide(own_ref), LANES))
    face_contract(
        lambda q, f: big[f * FACE_ROWS : (f + 1) * FACE_ROWS, q * LANES : (q + 1) * LANES],
        solver_ref, 0, flux,
    )
    lifted = matmul(lift_ref[...], stacked(flux[...], 192))
    def finish(p, total):
        change = total - lifted[:, p * LANES : (p + 1) * LANES]
        base_ref[p] = state_ref[p] + jnp.where(ending, change, 0.0)

    contract_star(big, FACES * FACE_ROWS, star_ref, finish)
    both = matmul(table_ref[...], local_ref[...])
    picked = both[:TABLE] + both[TABLE:]
    partial_ref[...] = picked if sum_ref is None else sum_ref[...] + picked


def own_first_kernel(
    state_ref, own_ref, table_ref, star_ref, solver_ref, period_ref,
    stiffness_ref, projection_ref, lifting_ref, neighbor_ref, order_ref,
    base_ref, partial_ref, both_ref, lift_ref, local_ref, remote_ref,
    big, flux, work, work_lift,
):
    work[...] = jnp.zeros_like(work)
    for f in range(FACES):
        weights_into(work, f * FACE_ROWS, projection_ref[f], ROWS)
    for d in range(3):
        weights_into(work, FACES * FACE_ROWS + d * ROWS, stiffness_ref[d].T, ROWS)
    both_ref[...] = work[...].astype(BF16)
    work_lift[...] = jnp.zeros_like(work_lift)
    lifts = jnp.zeros((BASIS, 192), F32)
    for f in range(FACES):
        high, low = split_pair(lifting_ref[f])
        for part, offset in ((high, 0), (high, 64), (low, 128)):
            lifts = lifts + placed(part, offset + f * FACE_ROWS, 192, 0)
    work_lift[0:BASIS, :] = lifts
    lift_ref[...] = work_lift[...].astype(BF16)
    column = lax.broadcasted_iota(jnp.int32, (LANES, LANES), 0)
    for f in range(FACES):
        row = neighbor_ref[f : f + 1, :]
        for g in range(6):
            chosen = (column + g * LANES == row).astype(F32).astype(BF16)
            if g < FACES:
                local_ref[g * LANES : (g + 1) * LANES, f * LANES : (f + 1) * LANES] = chosen
            else:
                start = (g - FACES) * LANES
                remote_ref[start : start + LANES, f * LANES : (f + 1) * LANES] = chosen
    own_body(
        0, state_ref, own_ref, table_ref, None, star_ref, solver_ref, period_ref,
        both_ref, lift_ref, local_ref, base_ref, partial_ref, big, flux,
    )


def own_kernel(
    tick, state_ref, own_ref, table_ref, sum_ref, star_ref, solver_ref, period_ref,
    both_ref, lift_ref, local_ref, order_ref,
    base_ref, partial_ref, big, flux,
):
    own_body(
        tick, state_ref, own_ref, table_ref, sum_ref, star_ref, solver_ref, period_ref,
        both_ref, lift_ref, local_ref, base_ref, partial_ref, big, flux,
    )


def near_body(
    tick, first_ref, second_ref, gathered_ref, base_ref, partial_ref, solver_ref, period_ref,
    lift_ref, remote_ref, sums, flux,
):
    me = lax.axis_index("region")
    core = lax.rem(me, 2)
    even = lax.rem(me // 2, 2) == 0
    lane = lax.broadcasted_iota(jnp.int32, (TABLE, LANES), 1)
    low_half = lane < LANES // 2
    partner = gathered_ref[1 - core]
    first, second = first_ref[...], second_ref[...]
    upward = jnp.where(even, first, second)
    downward = jnp.where(even, second, first)
    lower = jnp.where(jnp.logical_and(core == 1, low_half), partner, upward)
    upper = jnp.where(
        jnp.logical_and(core == 0, jnp.logical_not(low_half)), partner, downward
    )
    high, low = split_pair(jnp.concatenate([lower, upper], axis=1))
    both = matmul(jnp.concatenate([high, low], axis=0), remote_ref[...])
    sums[...] = partial_ref[...] + both[:TABLE] + both[TABLE:]
    face_contract(
        lambda q, f: sums[q * FACE_ROWS : (q + 1) * FACE_ROWS, f * LANES : (f + 1) * LANES],
        solver_ref, 1, flux,
    )
    return matmul(lift_ref[...], stacked(flux[...], 192))


def step_kernel(
    tick, first_ref, second_ref, gathered_ref, base_ref, partial_ref, star_ref, solver_ref,
    period_ref, lift_ref, remote_ref, stiff_ref, proj_ref, send_ref,
    state_ref, sum_ref, own_ref, table_ref, near_list_ref, far_list_ref,
    sums, flux, derivs, blocks, faces,
):
    lifted = near_body(
        tick, first_ref, second_ref, gathered_ref, base_ref, partial_ref, solver_ref, period_ref,
        lift_ref, remote_ref, sums, flux,
    )
    ending = ending_mask(period_ref[0:1, :], tick)
    for p in range(NQ):
        change = jnp.where(ending, lifted[:, p * LANES : (p + 1) * LANES], 0.0)
        value = base_ref[p] - change
        derivs[0, p] = value
        state_ref[p] = value
    for f in range(FACES):
        part = sums[:, f * LANES : (f + 1) * LANES]
        sum_ref[:, f * LANES : (f + 1) * LANES] = jnp.where(ending, 0.0, part)
    predict_and_send(
        tick + 1, None, star_ref, stiff_ref, proj_ref, send_ref, period_ref,
        table_ref, own_ref, near_list_ref, far_list_ref, derivs, blocks, faces,
    )


def end_kernel(
    first_ref, second_ref, gathered_ref, base_ref, partial_ref, solver_ref,
    period_ref, lift_ref, remote_ref,
    out_ref, sums, flux,
):
    tick = TICKS - 1
    lifted = near_body(
        tick, first_ref, second_ref, gathered_ref, base_ref, partial_ref, solver_ref, period_ref,
        lift_ref, remote_ref, sums, flux,
    )
    ending = ending_mask(period_ref[0:1, :], tick)
    for p in range(NQ):
        change = jnp.where(ending, lifted[:, p * LANES : (p + 1) * LANES], 0.0)
        out_ref[p] = (base_ref[p] - change)[0:BASIS, :]


VMEM = pl.BlockSpec(memory_space=pltpu.VMEM)
SMEM = pl.BlockSpec(memory_space=pltpu.SMEM)


def call(kernel, name, inputs, outputs, scratch, flops, in_specs=None):
    return pl.pallas_call(
        kernel,
        name=name,
        out_shape=[jax.ShapeDtypeStruct(s, d) for s, d in outputs],
        in_specs=in_specs or [VMEM] * len(inputs),
        out_specs=[VMEM] * len(outputs),
        scratch_shapes=[pltpu.VMEM(s, d) for s, d in scratch],
        cost_estimate=pl.CostEstimate(flops=flops, bytes_accessed=flops // 100, transcendentals=0),
        compiler_params=pltpu.CompilerParams(vmem_limit_bytes=24 << 20),
    )(*inputs)


STATE = ((NQ, ROWS, LANES), F32)
PAIRED = ((2 * TABLE, FACES * LANES), BF16)
SUMS = ((TABLE, FACES * LANES), F32)
LIST = ((TABLE, LANES), F32)
DERIV = ((DERIVS, NQ, ROWS, LANES), F32)
BLOCKS = ((3 * ROWS, WIDE), F32)
FACE = ((FACES * FACE_ROWS, WIDE), F32)
BOTH_ROWS = FACES * FACE_ROWS + 3 * ROWS
BIG = ((BOTH_ROWS, WIDE), F32)


def per_device(
    coefficients, star, solvers, stiffness, projection, lifting, block_cluster, neighbors, send_faces
):
    count = lax.axis_size("region")
    cores = [[2 * k, 2 * k + 1] for k in range(count // 2)]
    pairs = ([], [])
    for i in range(count - 2):
        pairs[(i // 2) % 2] .extend([(i, i + 2), (i + 2, i)])
    inner, outer = pairs

    (state, own, table, near_list, far_list, stiff_w, proj_w, send_w, period) = call(
        begin_kernel, "begin",
        (coefficients, star, stiffness, projection, block_cluster, send_faces),
        (
            STATE, STATE, PAIRED, LIST, LIST,
            ((3 * ROWS, LANES), BF16), ((FACES * FACE_ROWS, LANES), BF16),
            ((FACES * LANES, 2 * LANES), BF16), ((8, LANES), jnp.int32),
        ),
        (DERIV, BLOCKS, FACE, ((3 * ROWS, LANES), F32)),
        10**9,
        [VMEM, VMEM, VMEM, VMEM, SMEM, VMEM],
    )
    sums = None
    for tick in range(TICKS):
        gathered = lax.all_gather(near_list, "region", axis_index_groups=cores)
        first, second = call(
            relay_kernel, "relay", (gathered, far_list), (LIST, LIST), (), 10**6
        )
        first_in = lax.ppermute(first, "region", outer)
        second_in = lax.ppermute(second, "region", inner)
        if tick == 0:
            base, partial, both_w, lift_w, local_w, remote_w = call(
                own_first_kernel, "own_first",
                (
                    state, own, table, star, solvers, period,
                    stiffness, projection, lifting, neighbors, first[:8],
                ),
                (
                    STATE, SUMS, ((BOTH_ROWS, LANES), BF16), ((ROWS, 192), BF16),
                    ((FACES * LANES, FACES * LANES), BF16), ((2 * LANES, FACES * LANES), BF16),
                ),
                (BIG, FACE, ((BOTH_ROWS, LANES), F32), ((ROWS, 192), F32)),
                10**9,
            )
        else:
            base, partial = call(
                functools.partial(own_kernel, tick), "own",
                (state, own, table, sums, star, solvers, period, both_w, lift_w, local_w, first[:8]),
                (STATE, SUMS), (BIG, FACE), 10**9,
            )
        if tick < TICKS - 1:
            state, sums, own, table, near_list, far_list = call(
                functools.partial(step_kernel, tick), "step",
                (
                    first_in, second_in, gathered, base, partial, star, solvers,
                    period, lift_w, remote_w, stiff_w, proj_w, send_w,
                ),
                (STATE, SUMS, STATE, PAIRED, LIST, LIST),
                (SUMS, FACE, DERIV, BLOCKS, FACE), 10**9,
            )
    (updated,) = call(
        end_kernel, "end",
        (first_in, second_in, gathered, base, partial, solvers, period, lift_w, remote_w),
        (((NQ, BASIS, LANES), F32),), (SUMS, FACE), 10**9,
    )
    return updated


def solution(mesh):
    placed_specs = (
        P(None, None, "region"),
        P(None, None, None, "region"),
        P(None, None, None, None, "region"),
        P(),
        P(),
        P(),
        P("region"),
        P(None, "region"),
        P(None, "region"),
    )
    return jax.shard_map(
        per_device, mesh=mesh, in_specs=placed_specs, out_specs=P(None, None, "region"),
        check_vma=False,
    )
```

```python
import functools

import jax
import jax.numpy as jnp
from jax import lax
from jax.experimental import pallas as pl
from jax.experimental.pallas import tpu as pltpu
from jax.sharding import PartitionSpec as P

NQ = 9
BASIS = 35
ROWS = 40
FACES = 4
FACE_BASIS = 15
FACE_ROWS = 16
DERIVS = 5
TICKS = 4
LANES = 128
STEP = 0.125
FACTORIALS = (1.0, 2.0, 6.0, 24.0, 120.0)
F32 = jnp.float32
BF16 = jnp.bfloat16
TABLE = NQ * FACE_ROWS
WIDE = NQ * LANES


def split_pair(x):
    high = x.astype(BF16)
    return high, (x - high.astype(F32)).astype(BF16)


def stacked(x, depth):
    high = x.astype(BF16).astype(F32)
    parts = [high, x - high, high]
    rest = depth - 3 * x.shape[0]
    if rest:
        parts.append(jnp.zeros((rest, x.shape[1]), F32))
    return jnp.concatenate(parts, axis=0).astype(BF16)


def placed(block, offset, width, rows):
    source = lax.broadcasted_iota(jnp.int32, (block.shape[1], width), 0)
    target = lax.broadcasted_iota(jnp.int32, (block.shape[1], width), 1)
    chosen = (target == source + offset).astype(BF16)
    return jnp.dot(block, chosen, preferred_element_type=F32)


def weights_into(ref, row, block, stride):
    high, low = split_pair(block)
    width = ref.shape[1]
    full = (
        placed(high, 0, width, 0) + placed(high, stride, width, 0) + placed(low, 2 * stride, width, 0)
    )
    ref[row : row + block.shape[0], :] = full


def wide(ref):
    return jnp.concatenate([ref[q] for q in range(NQ)], axis=1)


def matmul(weights, x):
    return jnp.dot(weights, x, preferred_element_type=F32)


def contract_star(blocks, base, star_ref, finish):
    for start, size in ((0, 16), (16, 16), (32, 8)):
        partial = [None] * NQ
        for direction in range(3):
            row = base + direction * ROWS + start
            totals = [None] * NQ
            for source in range(NQ):
                block = blocks[row : row + size, source * LANES : (source + 1) * LANES]
                for p in range(NQ):
                    term = block * star_ref[direction, source, p : p + 1, :]
                    totals[p] = term if totals[p] is None else totals[p] + term
            for p in range(NQ):
                partial[p] = totals[p] if partial[p] is None else partial[p] + totals[p]
        for p in range(NQ):
            finish(p, slice(start, start + size), partial[p])


def tick_weights(period, tick):
    out = []
    for k in range(DERIVS):
        values = []
        for p in (1, 2, 4):
            s = STEP * (tick % p)
            values.append(((s + STEP) ** (k + 1) - s ** (k + 1)) / FACTORIALS[k])
        out.append(jnp.where(period == 1, values[0], jnp.where(period == 2, values[1], values[2])))
    return out


def own_weights(period):
    out = []
    for k in range(DERIVS):
        values = [(STEP * p) ** (k + 1) / FACTORIALS[k] for p in (1, 2, 4)]
        out.append(jnp.where(period == 1, values[0], jnp.where(period == 2, values[1], values[2])))
    return out


def weighted(derivs, q, weights):
    total = derivs[0, q] * weights[0]
    for k in range(1, DERIVS):
        total = total + derivs[k, q] * weights[k]
    return total


def predict_and_send(
    tick, star_ref, stiff_ref, proj_ref, send_ref, period_ref,
    derivs, table_ref, near_list_ref, far_list_ref, blocks, faces,
):
    def degree(k, carry):
        x = jnp.concatenate([derivs[k, q] for q in range(NQ)], axis=1)
        blocks[...] = matmul(stiff_ref[...], stacked(x, LANES))

        def finish(p, rows, total):
            derivs[k + 1, p, rows, :] = total

        contract_star(blocks, 0, star_ref, finish)
        return carry

    for k in range(DERIVS - 1):
        degree(k, 0)
    period = period_ref[0:1, :]
    now = tick_weights(period, tick)
    parts = []
    for q in range(NQ):
        parts.append(weighted(derivs, q, now))
    faces[...] = matmul(proj_ref[...], stacked(jnp.concatenate(parts, axis=1), LANES))
    highs, lows = [], []
    for q in range(NQ):
        row = jnp.concatenate(
            [
                faces[f * FACE_ROWS : (f + 1) * FACE_ROWS, q * LANES : (q + 1) * LANES]
                for f in range(FACES)
            ],
            axis=1,
        )
        high, low = split_pair(row)
        table_ref[q * FACE_ROWS : (q + 1) * FACE_ROWS, :] = high
        table_ref[TABLE + q * FACE_ROWS : TABLE + (q + 1) * FACE_ROWS, :] = low
    both = matmul(table_ref[...], send_ref[...])
    picked = both[:TABLE] + both[TABLE:]
    near_list_ref[...] = picked[:, :LANES]
    far_list_ref[...] = picked[:, LANES:]


def begin_kernel(
    coef_ref, star_ref, stiffness_ref, projection_ref, cluster_ref, faces_ref,
    derivs, table_ref, near_list_ref, far_list_ref,
    stiff_ref, proj_ref, send_ref, period_ref,
    blocks, faces, work,
):
    lane = lax.broadcasted_iota(jnp.int32, (8, LANES), 1)
    period = jnp.full((8, LANES), 1, jnp.int32)
    for j in range(LANES // 16):
        c = cluster_ref[j]
        p = jnp.where(c == 0, 1, jnp.where(c == 1, 2, 4))
        period = jnp.where((lane >> 4) == j, p, period)
    period_ref[...] = period
    derivs[0] = jnp.zeros((NQ, ROWS, LANES), F32)
    for q in range(NQ):
        derivs[0, q, 0:BASIS, :] = coef_ref[q]
    work[...] = jnp.zeros_like(work)
    for d in range(3):
        weights_into(work, d * ROWS, -stiffness_ref[d], ROWS)
    stiff_ref[...] = work[0 : 3 * ROWS, :].astype(BF16)
    work[...] = jnp.zeros_like(work)
    for f in range(FACES):
        weights_into(work, f * FACE_ROWS, projection_ref[:, f, :], ROWS)
    proj_ref[...] = work[0 : FACES * FACE_ROWS, :].astype(BF16)
    column = lax.broadcasted_iota(jnp.int32, (FACES * LANES, LANES), 0)
    near = jnp.concatenate([faces_ref[3:4, :], faces_ref[0:1, :]], axis=1)
    far = jnp.concatenate([faces_ref[1:2, :], faces_ref[2:3, :]], axis=1)
    send_ref[:, :LANES] = (column == near).astype(F32).astype(BF16)
    send_ref[:, LANES:] = (column == far).astype(F32).astype(BF16)
    predict_and_send(
        0, star_ref, stiff_ref, proj_ref, send_ref, period_ref,
        derivs, table_ref, near_list_ref, far_list_ref, blocks, faces,
    )


def relay_kernel(gathered_ref, far_list_ref, first_ref, second_ref):
    me = lax.axis_index("region")
    other = 1 - lax.rem(me, 2)
    even = lax.rem(me // 2, 2) == 0
    lane = lax.broadcasted_iota(jnp.int32, (TABLE, LANES), 1)
    partner = gathered_ref[other]
    own = far_list_ref[...]
    upward = jnp.where(lane < LANES // 2, partner, own)
    downward = jnp.where(lane < LANES // 2, own, partner)
    first_ref[...] = jnp.where(even, downward, upward)
    second_ref[...] = jnp.where(even, upward, downward)


def face_contract(source, solver_ref, side, into):
    for f in range(FACES):
        totals = [None] * NQ
        for q in range(NQ):
            block = source(q, f)
            for p in range(NQ):
                term = block * solver_ref[side, f, q, p : p + 1, :]
                totals[p] = term if totals[p] is None else totals[p] + term
        for p in range(NQ):
            into[f * FACE_ROWS : (f + 1) * FACE_ROWS, p * LANES : (p + 1) * LANES] = totals[p]


def ending_mask(period, tick):
    return period <= ((tick + 1) & -(tick + 1))


def own_body(
    tick, derivs, table_ref, sum_ref, star_ref, solver_ref, period_ref,
    both_ref, lift_ref, local_ref, base_ref, partial_ref, big, flux,
):
    period = period_ref[0:1, :]
    ending = ending_mask(period, tick)
    whole = own_weights(period)
    own = jnp.concatenate([weighted(derivs, q, whole) for q in range(NQ)], axis=1)
    big[...] = matmul(both_ref[...], stacked(own, LANES))
    face_contract(
        lambda q, f: big[f * FACE_ROWS : (f + 1) * FACE_ROWS, q * LANES : (q + 1) * LANES],
        solver_ref, 0, flux,
    )
    lifted = matmul(lift_ref[...], stacked(flux[...], 192))
    for p in range(NQ):
        base_ref[p] = lifted[:, p * LANES : (p + 1) * LANES]

    def finish(p, rows, total):
        change = total - base_ref[p, rows, :]
        base_ref[p, rows, :] = derivs[0, p, rows, :] + jnp.where(ending, change, 0.0)

    contract_star(big, FACES * FACE_ROWS, star_ref, finish)
    both = matmul(table_ref[...], local_ref[...])
    picked = both[:TABLE] + both[TABLE:]
    if sum_ref is None:
        partial_ref[...] = picked
    else:
        cleared = ending_mask(period, tick - 1)
        for f in range(FACES):
            where = slice(f * LANES, (f + 1) * LANES)
            partial_ref[:, where] = picked[:, where] + jnp.where(cleared, 0.0, sum_ref[:, where])


def own_first_kernel(
    derivs, table_ref, star_ref, solver_ref, period_ref,
    stiffness_ref, projection_ref, lifting_ref, neighbor_ref, order_ref,
    base_ref, partial_ref, both_ref, lift_ref, local_ref, remote_ref,
    big, flux, work, work_lift,
):
    work[...] = jnp.zeros_like(work)
    for f in range(FACES):
        weights_into(work, f * FACE_ROWS, projection_ref[:, f, :], ROWS)
    for d in range(3):
        weights_into(work, FACES * FACE_ROWS + d * ROWS, stiffness_ref[d].T, ROWS)
    both_ref[...] = work[...].astype(BF16)
    work_lift[...] = jnp.zeros_like(work_lift)
    lifts = jnp.zeros((BASIS, 192), F32)
    for f in range(FACES):
        high, low = split_pair(lifting_ref[f])
        for part, offset in ((high, 0), (high, 64), (low, 128)):
            lifts = lifts + placed(part, offset + f * FACE_ROWS, 192, 0)
    work_lift[0:BASIS, :] = lifts
    lift_ref[...] = work_lift[...].astype(BF16)
    column = lax.broadcasted_iota(jnp.int32, (LANES, LANES), 0)
    for f in range(FACES):
        row = neighbor_ref[f : f + 1, :]
        for g in range(6):
            chosen = (column + g * LANES == row).astype(F32).astype(BF16)
            if g < FACES:
                local_ref[g * LANES : (g + 1) * LANES, f * LANES : (f + 1) * LANES] = chosen
            else:
                start = (g - FACES) * LANES
                remote_ref[start : start + LANES, f * LANES : (f + 1) * LANES] = chosen
    own_body(
        0, derivs, table_ref, None, star_ref, solver_ref, period_ref,
        both_ref, lift_ref, local_ref, base_ref, partial_ref, big, flux,
    )


def own_kernel(
    tick, derivs, table_ref, sum_ref, star_ref, solver_ref, period_ref,
    both_ref, lift_ref, local_ref, order_ref,
    base_ref, partial_ref, big, flux,
):
    own_body(
        tick, derivs, table_ref, sum_ref, star_ref, solver_ref, period_ref,
        both_ref, lift_ref, local_ref, base_ref, partial_ref, big, flux,
    )


def near_body(
    tick, first_ref, second_ref, gathered_ref, base_ref, partial_ref, solver_ref, period_ref,
    lift_ref, remote_ref, sums, flux,
):
    me = lax.axis_index("region")
    core = lax.rem(me, 2)
    even = lax.rem(me // 2, 2) == 0
    lane = lax.broadcasted_iota(jnp.int32, (TABLE, LANES), 1)
    low_half = lane < LANES // 2
    partner = gathered_ref[1 - core]
    first, second = first_ref[...], second_ref[...]
    upward = jnp.where(even, first, second)
    downward = jnp.where(even, second, first)
    lower = jnp.where(jnp.logical_and(core == 1, low_half), partner, upward)
    upper = jnp.where(
        jnp.logical_and(core == 0, jnp.logical_not(low_half)), partner, downward
    )
    high, low = split_pair(jnp.concatenate([lower, upper], axis=1))
    both = matmul(jnp.concatenate([high, low], axis=0), remote_ref[...])
    sums[...] = partial_ref[...] + both[:TABLE] + both[TABLE:]
    face_contract(
        lambda q, f: sums[q * FACE_ROWS : (q + 1) * FACE_ROWS, f * LANES : (f + 1) * LANES],
        solver_ref, 1, flux,
    )
    return matmul(lift_ref[...], stacked(flux[...], 192))


def step_kernel(
    tick, first_ref, second_ref, gathered_ref, base_ref, partial_ref, star_ref, solver_ref,
    period_ref, lift_ref, remote_ref, stiff_ref, proj_ref, send_ref,
    derivs, sums, table_ref, near_list_ref, far_list_ref,
    flux, blocks, faces,
):
    lifted = near_body(
        tick, first_ref, second_ref, gathered_ref, base_ref, partial_ref, solver_ref, period_ref,
        lift_ref, remote_ref, sums, flux,
    )
    ending = ending_mask(period_ref[0:1, :], tick)
    for p in range(NQ):
        change = jnp.where(ending, lifted[:, p * LANES : (p + 1) * LANES], 0.0)
        value = base_ref[p] - change
        derivs[0, p] = value
    predict_and_send(
        tick + 1, star_ref, stiff_ref, proj_ref, send_ref, period_ref,
        derivs, table_ref, near_list_ref, far_list_ref, blocks, faces,
    )


def end_kernel(
    first_ref, second_ref, gathered_ref, base_ref, partial_ref, solver_ref,
    period_ref, lift_ref, remote_ref,
    out_ref, sums, flux,
):
    tick = TICKS - 1
    lifted = near_body(
        tick, first_ref, second_ref, gathered_ref, base_ref, partial_ref, solver_ref, period_ref,
        lift_ref, remote_ref, sums, flux,
    )
    ending = ending_mask(period_ref[0:1, :], tick)
    for p in range(NQ):
        change = jnp.where(ending, lifted[:, p * LANES : (p + 1) * LANES], 0.0)
        out_ref[p] = (base_ref[p] - change)[0:BASIS, :]


VMEM = pl.BlockSpec(memory_space=pltpu.VMEM)
SMEM = pl.BlockSpec(memory_space=pltpu.SMEM)


def call(kernel, name, inputs, outputs, scratch, flops, in_specs=None):
    return pl.pallas_call(
        kernel,
        name=name,
        out_shape=[jax.ShapeDtypeStruct(s, d) for s, d in outputs],
        in_specs=in_specs or [VMEM] * len(inputs),
        out_specs=[VMEM] * len(outputs),
        scratch_shapes=[pltpu.VMEM(s, d) for s, d in scratch],
        cost_estimate=pl.CostEstimate(flops=flops, bytes_accessed=flops // 100, transcendentals=0),
        compiler_params=pltpu.CompilerParams(vmem_limit_bytes=24 << 20),
    )(*inputs)


STATE = ((NQ, ROWS, LANES), F32)
PAIRED = ((2 * TABLE, FACES * LANES), BF16)
SUMS = ((TABLE, FACES * LANES), F32)
LIST = ((TABLE, LANES), F32)
DERIV = ((DERIVS, NQ, ROWS, LANES), F32)
BLOCKS = ((3 * ROWS, WIDE), F32)
FACE = ((FACES * FACE_ROWS, WIDE), F32)
BOTH_ROWS = FACES * FACE_ROWS + 3 * ROWS
BIG = ((BOTH_ROWS, WIDE), F32)


def per_device(
    coefficients, star, solvers, stiffness, projection, lifting, block_cluster, neighbors, send_faces
):
    projection = jnp.transpose(projection, (1, 0, 2))
    count = lax.axis_size("region")
    cores = [[2 * k, 2 * k + 1] for k in range(count // 2)]
    pairs = ([], [])
    for i in range(count - 2):
        pairs[(i // 2) % 2] .extend([(i, i + 2), (i + 2, i)])
    inner, outer = pairs

    (derivs, table, near_list, far_list, stiff_w, proj_w, send_w, period) = call(
        begin_kernel, "begin",
        (coefficients, star, stiffness, projection, block_cluster, send_faces),
        (
            DERIV, PAIRED, LIST, LIST,
            ((3 * ROWS, LANES), BF16), ((FACES * FACE_ROWS, LANES), BF16),
            ((FACES * LANES, 2 * LANES), BF16), ((8, LANES), jnp.int32),
        ),
        (BLOCKS, FACE, ((3 * ROWS, LANES), F32)),
        10**9,
        [VMEM, VMEM, VMEM, VMEM, SMEM, VMEM],
    )
    sums = None
    for tick in range(TICKS):
        gathered = lax.all_gather(near_list, "region", axis_index_groups=cores)
        first, second = call(
            relay_kernel, "relay", (gathered, far_list), (LIST, LIST), (), 10**6
        )
        first_in = lax.ppermute(first, "region", outer)
        second_in = lax.ppermute(second, "region", inner)
        if tick == 0:
            base, partial, both_w, lift_w, local_w, remote_w = call(
                own_first_kernel, "own_first",
                (
                    derivs, table, star, solvers, period,
                    stiffness, projection, lifting, neighbors, first[:8],
                ),
                (
                    STATE, SUMS, ((BOTH_ROWS, LANES), BF16), ((ROWS, 192), BF16),
                    ((FACES * LANES, FACES * LANES), BF16), ((2 * LANES, FACES * LANES), BF16),
                ),
                (BIG, FACE, ((BOTH_ROWS, LANES), F32), ((ROWS, 192), F32)),
                10**9,
            )
        else:
            base, partial = call(
                functools.partial(own_kernel, tick), "own",
                (derivs, table, sums, star, solvers, period, both_w, lift_w, local_w, first[:8]),
                (STATE, SUMS), (BIG, FACE), 10**9,
            )
        if tick < TICKS - 1:
            derivs, sums, table, near_list, far_list = call(
                functools.partial(step_kernel, tick), "step",
                (
                    first_in, second_in, gathered, base, partial, star, solvers,
                    period, lift_w, remote_w, stiff_w, proj_w, send_w,
                ),
                (DERIV, SUMS, PAIRED, LIST, LIST),
                (FACE, BLOCKS, FACE), 10**9,
            )
    (updated,) = call(
        end_kernel, "end",
        (first_in, second_in, gathered, base, partial, solvers, period, lift_w, remote_w),
        (((NQ, BASIS, LANES), F32),), (SUMS, FACE), 10**9,
    )
    return updated


def solution(mesh):
    placed_specs = (
        P(None, None, "region"),
        P(None, None, None, "region"),
        P(None, None, None, None, "region"),
        P(),
        P(),
        P(),
        P("region"),
        P(None, "region"),
        P(None, "region"),
    )
    return jax.shard_map(
        per_device, mesh=mesh, in_specs=placed_specs, out_specs=P(None, None, "region"),
        check_vma=False,
    )
```

```python
import functools

import jax
import jax.numpy as jnp
from jax import lax
from jax.experimental import pallas as pl
from jax.experimental.pallas import tpu as pltpu
from jax.sharding import PartitionSpec as P

NQ = 9
BASIS = 35
ROWS = 40
FACES = 4
FACE_BASIS = 15
FACE_ROWS = 16
DERIVS = 5
TICKS = 4
LANES = 128
STEP = 0.125
FACTORIALS = (1.0, 2.0, 6.0, 24.0, 120.0)
F32 = jnp.float32
BF16 = jnp.bfloat16
TABLE = NQ * FACE_ROWS
WIDE = NQ * LANES


def split_pair(x):
    high = x.astype(BF16)
    return high, (x - high.astype(F32)).astype(BF16)


def stacked(x, depth):
    high = x.astype(BF16).astype(F32)
    parts = [high, x - high, high]
    rest = depth - 3 * x.shape[0]
    if rest:
        parts.append(jnp.zeros((rest, x.shape[1]), F32))
    return jnp.concatenate(parts, axis=0).astype(BF16)


def placed(block, offset, width, rows):
    source = lax.broadcasted_iota(jnp.int32, (block.shape[1], width), 0)
    target = lax.broadcasted_iota(jnp.int32, (block.shape[1], width), 1)
    chosen = (target == source + offset).astype(BF16)
    return jnp.dot(block, chosen, preferred_element_type=F32)


def weights_into(ref, row, block, stride):
    high, low = split_pair(block)
    width = ref.shape[1]
    full = (
        placed(high, 0, width, 0) + placed(high, stride, width, 0) + placed(low, 2 * stride, width, 0)
    )
    ref[row : row + block.shape[0], :] = full


def wide(ref):
    return jnp.concatenate([ref[q] for q in range(NQ)], axis=1)


def matmul(weights, x):
    return jnp.dot(weights, x, preferred_element_type=F32)


def contract_star(blocks, base, star_ref, finish):
    for start, size in ((0, 16), (16, 16), (32, 8)):
        partial = [None] * NQ
        for direction in range(3):
            row = base + direction * ROWS + start
            totals = [None] * NQ
            for source in range(NQ):
                block = blocks[row : row + size, source * LANES : (source + 1) * LANES]
                for p in range(NQ):
                    term = block * star_ref[direction, source, p : p + 1, :]
                    totals[p] = term if totals[p] is None else totals[p] + term
            for p in range(NQ):
                partial[p] = totals[p] if partial[p] is None else partial[p] + totals[p]
        for p in range(NQ):
            finish(p, slice(start, start + size), partial[p])


def tick_weights(period, tick):
    out = []
    for k in range(DERIVS):
        values = []
        for p in (1, 2, 4):
            s = STEP * (tick % p)
            values.append(((s + STEP) ** (k + 1) - s ** (k + 1)) / FACTORIALS[k])
        out.append(jnp.where(period == 1, values[0], jnp.where(period == 2, values[1], values[2])))
    return out


def own_weights(period):
    out = []
    for k in range(DERIVS):
        values = [(STEP * p) ** (k + 1) / FACTORIALS[k] for p in (1, 2, 4)]
        out.append(jnp.where(period == 1, values[0], jnp.where(period == 2, values[1], values[2])))
    return out


def weighted(derivs, q, weights):
    total = derivs[0, q] * weights[0]
    for k in range(1, DERIVS):
        total = total + derivs[k, q] * weights[k]
    return total


def predict_and_send(
    tick, star_ref, stiff_ref, proj_ref, send_ref, period_ref,
    derivs, table_ref, near_list_ref, far_list_ref, blocks, faces,
):
    def degree(k, carry):
        x = jnp.concatenate([derivs[k, q] for q in range(NQ)], axis=1)
        blocks[...] = matmul(stiff_ref[...], stacked(x, LANES))

        def finish(p, rows, total):
            derivs[k + 1, p, rows, :] = total

        contract_star(blocks, 0, star_ref, finish)
        return carry

    for k in range(DERIVS - 1):
        degree(k, 0)
    if tick == 0:
        now = [STEP ** (k + 1) / FACTORIALS[k] for k in range(DERIVS)]
    else:
        now = tick_weights(period_ref[0:1, :], tick)
    parts = []
    for q in range(NQ):
        parts.append(weighted(derivs, q, now))
    faces[...] = matmul(proj_ref[...], stacked(jnp.concatenate(parts, axis=1), LANES))
    highs, lows = [], []
    for q in range(NQ):
        row = jnp.concatenate(
            [
                faces[f * FACE_ROWS : (f + 1) * FACE_ROWS, q * LANES : (q + 1) * LANES]
                for f in range(FACES)
            ],
            axis=1,
        )
        high, low = split_pair(row)
        table_ref[q * FACE_ROWS : (q + 1) * FACE_ROWS, :] = high
        table_ref[TABLE + q * FACE_ROWS : TABLE + (q + 1) * FACE_ROWS, :] = low
    both = matmul(table_ref[...], send_ref[...])
    picked = both[:TABLE] + both[TABLE:]
    near_list_ref[...] = picked[:, :LANES]
    far_list_ref[...] = picked[:, LANES:]


def begin_kernel(
    coef_ref, star_ref, stiffness_ref, projection_ref, faces_ref,
    derivs, table_ref, near_list_ref, far_list_ref,
    stiff_ref, proj_ref, send_ref,
    blocks, faces, work,
):
    derivs[0] = jnp.zeros((NQ, ROWS, LANES), F32)
    for q in range(NQ):
        derivs[0, q, 0:BASIS, :] = coef_ref[q]
    work[...] = jnp.zeros_like(work)
    for d in range(3):
        weights_into(work, d * ROWS, -stiffness_ref[d], ROWS)
    stiff_ref[...] = work[0 : 3 * ROWS, :].astype(BF16)
    work[...] = jnp.zeros_like(work)
    for f in range(FACES):
        weights_into(work, f * FACE_ROWS, projection_ref[:, f, :], ROWS)
    proj_ref[...] = work[0 : FACES * FACE_ROWS, :].astype(BF16)
    column = lax.broadcasted_iota(jnp.int32, (FACES * LANES, LANES), 0)
    near = jnp.concatenate([faces_ref[3:4, :], faces_ref[0:1, :]], axis=1)
    far = jnp.concatenate([faces_ref[1:2, :], faces_ref[2:3, :]], axis=1)
    send_ref[:, :LANES] = (column == near).astype(F32).astype(BF16)
    send_ref[:, LANES:] = (column == far).astype(F32).astype(BF16)
    predict_and_send(
        0, star_ref, stiff_ref, proj_ref, send_ref, None,
        derivs, table_ref, near_list_ref, far_list_ref, blocks, faces,
    )


def relay_kernel(gathered_ref, far_list_ref, first_ref, second_ref):
    me = lax.axis_index("region")
    other = 1 - lax.rem(me, 2)
    even = lax.rem(me // 2, 2) == 0
    lane = lax.broadcasted_iota(jnp.int32, (TABLE, LANES), 1)
    partner = gathered_ref[other]
    own = far_list_ref[...]
    upward = jnp.where(lane < LANES // 2, partner, own)
    downward = jnp.where(lane < LANES // 2, own, partner)
    first_ref[...] = jnp.where(even, downward, upward)
    second_ref[...] = jnp.where(even, upward, downward)


def face_contract(source, solver_ref, side, into):
    for f in range(FACES):
        totals = [None] * NQ
        for q in range(NQ):
            block = source(q, f)
            for p in range(NQ):
                term = block * solver_ref[side, f, q, p : p + 1, :]
                totals[p] = term if totals[p] is None else totals[p] + term
        for p in range(NQ):
            into[f * FACE_ROWS : (f + 1) * FACE_ROWS, p * LANES : (p + 1) * LANES] = totals[p]


def ending_mask(period, tick):
    return period <= ((tick + 1) & -(tick + 1))


def own_body(
    tick, derivs, table_ref, sum_ref, star_ref, solver_ref, period_ref,
    both_ref, lift_ref, local_ref, base_ref, partial_ref, big, flux,
):
    period = period_ref[0:1, :]
    ending = ending_mask(period, tick)
    whole = own_weights(period)
    own = jnp.concatenate([weighted(derivs, q, whole) for q in range(NQ)], axis=1)
    big[...] = matmul(both_ref[...], stacked(own, LANES))
    face_contract(
        lambda q, f: big[f * FACE_ROWS : (f + 1) * FACE_ROWS, q * LANES : (q + 1) * LANES],
        solver_ref, 0, flux,
    )
    lifted = matmul(lift_ref[...], stacked(flux[...], 192))
    for p in range(NQ):
        base_ref[p] = lifted[:, p * LANES : (p + 1) * LANES]

    def finish(p, rows, total):
        change = total - base_ref[p, rows, :]
        base_ref[p, rows, :] = derivs[0, p, rows, :] + jnp.where(ending, change, 0.0)

    contract_star(big, FACES * FACE_ROWS, star_ref, finish)
    both = matmul(table_ref[...], local_ref[...])
    picked = both[:TABLE] + both[TABLE:]
    if sum_ref is None:
        partial_ref[...] = picked
    else:
        cleared = ending_mask(period, tick - 1)
        for f in range(FACES):
            where = slice(f * LANES, (f + 1) * LANES)
            partial_ref[:, where] = picked[:, where] + jnp.where(cleared, 0.0, sum_ref[:, where])


def own_first_kernel(
    derivs, table_ref, star_ref, solver_ref, cluster_ref,
    stiffness_ref, projection_ref, lifting_ref, neighbor_ref, order_ref,
    base_ref, partial_ref, both_ref, lift_ref, local_ref, remote_ref, period_ref,
    big, flux, work, work_lift,
):
    lane = lax.broadcasted_iota(jnp.int32, (8, LANES), 1)
    period = jnp.full((8, LANES), 1, jnp.int32)
    for j in range(LANES // 16):
        c = cluster_ref[j]
        p = jnp.where(c == 0, 1, jnp.where(c == 1, 2, 4))
        period = jnp.where((lane >> 4) == j, p, period)
    period_ref[...] = period
    work[...] = jnp.zeros_like(work)
    for f in range(FACES):
        weights_into(work, f * FACE_ROWS, projection_ref[:, f, :], ROWS)
    for d in range(3):
        weights_into(work, FACES * FACE_ROWS + d * ROWS, stiffness_ref[d].T, ROWS)
    both_ref[...] = work[...].astype(BF16)
    work_lift[...] = jnp.zeros_like(work_lift)
    lifts = jnp.zeros((BASIS, 192), F32)
    for f in range(FACES):
        high, low = split_pair(lifting_ref[f])
        for part, offset in ((high, 0), (high, 64), (low, 128)):
            lifts = lifts + placed(part, offset + f * FACE_ROWS, 192, 0)
    work_lift[0:BASIS, :] = lifts
    lift_ref[...] = work_lift[...].astype(BF16)
    column = lax.broadcasted_iota(jnp.int32, (LANES, LANES), 0)
    for f in range(FACES):
        row = neighbor_ref[f : f + 1, :]
        for g in range(6):
            chosen = (column + g * LANES == row).astype(F32).astype(BF16)
            if g < FACES:
                local_ref[g * LANES : (g + 1) * LANES, f * LANES : (f + 1) * LANES] = chosen
            else:
                start = (g - FACES) * LANES
                remote_ref[start : start + LANES, f * LANES : (f + 1) * LANES] = chosen
    own_body(
        0, derivs, table_ref, None, star_ref, solver_ref, period_ref,
        both_ref, lift_ref, local_ref, base_ref, partial_ref, big, flux,
    )


def own_kernel(
    tick, derivs, table_ref, sum_ref, star_ref, solver_ref, period_ref,
    both_ref, lift_ref, local_ref, order_ref,
    base_ref, partial_ref, big, flux,
):
    own_body(
        tick, derivs, table_ref, sum_ref, star_ref, solver_ref, period_ref,
        both_ref, lift_ref, local_ref, base_ref, partial_ref, big, flux,
    )


def near_body(
    tick, first_ref, second_ref, gathered_ref, base_ref, partial_ref, solver_ref, period_ref,
    lift_ref, remote_ref, sums, flux,
):
    me = lax.axis_index("region")
    core = lax.rem(me, 2)
    even = lax.rem(me // 2, 2) == 0
    lane = lax.broadcasted_iota(jnp.int32, (TABLE, LANES), 1)
    low_half = lane < LANES // 2
    partner = gathered_ref[1 - core]
    first, second = first_ref[...], second_ref[...]
    upward = jnp.where(even, first, second)
    downward = jnp.where(even, second, first)
    lower = jnp.where(jnp.logical_and(core == 1, low_half), partner, upward)
    upper = jnp.where(
        jnp.logical_and(core == 0, jnp.logical_not(low_half)), partner, downward
    )
    high, low = split_pair(jnp.concatenate([lower, upper], axis=1))
    both = matmul(jnp.concatenate([high, low], axis=0), remote_ref[...])
    sums[...] = partial_ref[...] + both[:TABLE] + both[TABLE:]
    face_contract(
        lambda q, f: sums[q * FACE_ROWS : (q + 1) * FACE_ROWS, f * LANES : (f + 1) * LANES],
        solver_ref, 1, flux,
    )
    return matmul(lift_ref[...], stacked(flux[...], 192))


def step_kernel(
    tick, first_ref, second_ref, gathered_ref, base_ref, partial_ref, star_ref, solver_ref,
    period_ref, lift_ref, remote_ref, stiff_ref, proj_ref, send_ref,
    derivs, sums, table_ref, near_list_ref, far_list_ref,
    flux, blocks, faces,
):
    lifted = near_body(
        tick, first_ref, second_ref, gathered_ref, base_ref, partial_ref, solver_ref, period_ref,
        lift_ref, remote_ref, sums, flux,
    )
    ending = ending_mask(period_ref[0:1, :], tick)
    for p in range(NQ):
        change = jnp.where(ending, lifted[:, p * LANES : (p + 1) * LANES], 0.0)
        value = base_ref[p] - change
        derivs[0, p] = value
    predict_and_send(
        tick + 1, star_ref, stiff_ref, proj_ref, send_ref, period_ref,
        derivs, table_ref, near_list_ref, far_list_ref, blocks, faces,
    )


def end_kernel(
    first_ref, second_ref, gathered_ref, base_ref, partial_ref, solver_ref,
    period_ref, lift_ref, remote_ref,
    out_ref, sums, flux,
):
    tick = TICKS - 1
    lifted = near_body(
        tick, first_ref, second_ref, gathered_ref, base_ref, partial_ref, solver_ref, period_ref,
        lift_ref, remote_ref, sums, flux,
    )
    ending = ending_mask(period_ref[0:1, :], tick)
    for p in range(NQ):
        change = jnp.where(ending, lifted[:, p * LANES : (p + 1) * LANES], 0.0)
        out_ref[p] = (base_ref[p] - change)[0:BASIS, :]


VMEM = pl.BlockSpec(memory_space=pltpu.VMEM)
SMEM = pl.BlockSpec(memory_space=pltpu.SMEM)


def call(kernel, name, inputs, outputs, scratch, flops, in_specs=None):
    return pl.pallas_call(
        kernel,
        name=name,
        out_shape=[jax.ShapeDtypeStruct(s, d) for s, d in outputs],
        in_specs=in_specs or [VMEM] * len(inputs),
        out_specs=[VMEM] * len(outputs),
        scratch_shapes=[pltpu.VMEM(s, d) for s, d in scratch],
        cost_estimate=pl.CostEstimate(flops=flops, bytes_accessed=flops // 100, transcendentals=0),
        compiler_params=pltpu.CompilerParams(vmem_limit_bytes=24 << 20),
    )(*inputs)


STATE = ((NQ, ROWS, LANES), F32)
PAIRED = ((2 * TABLE, FACES * LANES), BF16)
SUMS = ((TABLE, FACES * LANES), F32)
LIST = ((TABLE, LANES), F32)
DERIV = ((DERIVS, NQ, ROWS, LANES), F32)
BLOCKS = ((3 * ROWS, WIDE), F32)
FACE = ((FACES * FACE_ROWS, WIDE), F32)
BOTH_ROWS = FACES * FACE_ROWS + 3 * ROWS
BIG = ((BOTH_ROWS, WIDE), F32)


def per_device(
    coefficients, star, solvers, stiffness, projection, lifting, block_cluster, neighbors, send_faces
):
    projection = jnp.transpose(projection, (1, 0, 2))
    count = lax.axis_size("region")
    cores = [[2 * k, 2 * k + 1] for k in range(count // 2)]
    pairs = ([], [])
    for i in range(count - 2):
        pairs[(i // 2) % 2] .extend([(i, i + 2), (i + 2, i)])
    inner, outer = pairs

    (derivs, table, near_list, far_list, stiff_w, proj_w, send_w) = call(
        begin_kernel, "begin",
        (coefficients, star, stiffness, projection, send_faces),
        (
            DERIV, PAIRED, LIST, LIST,
            ((3 * ROWS, LANES), BF16), ((FACES * FACE_ROWS, LANES), BF16),
            ((FACES * LANES, 2 * LANES), BF16),
        ),
        (BLOCKS, FACE, ((3 * ROWS, LANES), F32)),
        10**9,
    )
    sums = None
    for tick in range(TICKS):
        gathered = lax.all_gather(near_list, "region", axis_index_groups=cores)
        first, second = call(
            relay_kernel, "relay", (gathered, far_list), (LIST, LIST), (), 10**6
        )
        first_in = lax.ppermute(first, "region", outer)
        second_in = lax.ppermute(second, "region", inner)
        if tick == 0:
            base, partial, both_w, lift_w, local_w, remote_w, period = call(
                own_first_kernel, "own_first",
                (
                    derivs, table, star, solvers, block_cluster,
                    stiffness, projection, lifting, neighbors, first[:8],
                ),
                (
                    STATE, SUMS, ((BOTH_ROWS, LANES), BF16), ((ROWS, 192), BF16),
                    ((FACES * LANES, FACES * LANES), BF16), ((2 * LANES, FACES * LANES), BF16),
                    ((8, LANES), jnp.int32),
                ),
                (BIG, FACE, ((BOTH_ROWS, LANES), F32), ((ROWS, 192), F32)),
                10**9,
                [VMEM] * 4 + [SMEM] + [VMEM] * 5,
            )
        else:
            base, partial = call(
                functools.partial(own_kernel, tick), "own",
                (derivs, table, sums, star, solvers, period, both_w, lift_w, local_w, first[:8]),
                (STATE, SUMS), (BIG, FACE), 10**9,
            )
        if tick < TICKS - 1:
            derivs, sums, table, near_list, far_list = call(
                functools.partial(step_kernel, tick), "step",
                (
                    first_in, second_in, gathered, base, partial, star, solvers,
                    period, lift_w, remote_w, stiff_w, proj_w, send_w,
                ),
                (DERIV, SUMS, PAIRED, LIST, LIST),
                (FACE, BLOCKS, FACE), 10**9,
            )
    (updated,) = call(
        end_kernel, "end",
        (first_in, second_in, gathered, base, partial, solvers, period, lift_w, remote_w),
        (((NQ, BASIS, LANES), F32),), (SUMS, FACE), 10**9,
    )
    return updated


def solution(mesh):
    placed_specs = (
        P(None, None, "region"),
        P(None, None, None, "region"),
        P(None, None, None, None, "region"),
        P(),
        P(),
        P(),
        P("region"),
        P(None, "region"),
        P(None, "region"),
    )
    return jax.shard_map(
        per_device, mesh=mesh, in_specs=placed_specs, out_specs=P(None, None, "region"),
        check_vma=False,
    )
```

```python
import functools

import jax
import jax.numpy as jnp
from jax import lax
from jax.experimental import pallas as pl
from jax.experimental.pallas import tpu as pltpu
from jax.sharding import PartitionSpec as P

NQ = 9
BASIS = 35
ROWS = 40
FACES = 4
FACE_BASIS = 15
FACE_ROWS = 16
DERIVS = 5
TICKS = 4
LANES = 128
STEP = 0.125
FACTORIALS = (1.0, 2.0, 6.0, 24.0, 120.0)
F32 = jnp.float32
BF16 = jnp.bfloat16
TABLE = NQ * FACE_ROWS
WIDE = NQ * LANES


def split_pair(x):
    high = x.astype(BF16)
    return high, (x - high.astype(F32)).astype(BF16)


def stacked(x, depth):
    high = x.astype(BF16).astype(F32)
    parts = [high, x - high, high]
    rest = depth - 3 * x.shape[0]
    if rest:
        parts.append(jnp.zeros((rest, x.shape[1]), F32))
    return jnp.concatenate(parts, axis=0).astype(BF16)


def placed(block, offset, width, rows):
    source = lax.broadcasted_iota(jnp.int32, (block.shape[1], width), 0)
    target = lax.broadcasted_iota(jnp.int32, (block.shape[1], width), 1)
    chosen = (target == source + offset).astype(BF16)
    return jnp.dot(block, chosen, preferred_element_type=F32)


def weights_into(ref, row, block, stride):
    high, low = split_pair(block)
    width = ref.shape[1]
    full = (
        placed(high, 0, width, 0) + placed(high, stride, width, 0) + placed(low, 2 * stride, width, 0)
    )
    ref[row : row + block.shape[0], :] = full


def wide(ref):
    return jnp.concatenate([ref[q] for q in range(NQ)], axis=1)


def matmul(weights, x):
    return jnp.dot(weights, x, preferred_element_type=F32)


def contract_star(blocks, base, star_ref, finish):
    for start, size in ((0, 16), (16, 16), (32, 8)):
        partial = [None] * NQ
        for direction in range(3):
            row = base + direction * ROWS + start
            totals = [None] * NQ
            for source in range(NQ):
                block = blocks[row : row + size, source * LANES : (source + 1) * LANES]
                for p in range(NQ):
                    term = block * star_ref[direction, source, p : p + 1, :]
                    totals[p] = term if totals[p] is None else totals[p] + term
            for p in range(NQ):
                partial[p] = totals[p] if partial[p] is None else partial[p] + totals[p]
        for p in range(NQ):
            finish(p, slice(start, start + size), partial[p])


def tick_weights(period, tick):
    out = []
    for k in range(DERIVS):
        values = []
        for p in (1, 2, 4):
            s = STEP * (tick % p)
            values.append(((s + STEP) ** (k + 1) - s ** (k + 1)) / FACTORIALS[k])
        out.append(jnp.where(period == 1, values[0], jnp.where(period == 2, values[1], values[2])))
    return out


def own_weights(period):
    out = []
    for k in range(DERIVS):
        values = [(STEP * p) ** (k + 1) / FACTORIALS[k] for p in (1, 2, 4)]
        out.append(jnp.where(period == 1, values[0], jnp.where(period == 2, values[1], values[2])))
    return out


def weighted(derivs, q, weights):
    total = derivs[0, q] * weights[0]
    for k in range(1, DERIVS):
        total = total + derivs[k, q] * weights[k]
    return total


def predict_and_send(
    tick, star_ref, stiff_ref, proj_ref, send_ref, period_ref,
    derivs, table_ref, near_list_ref, far_list_ref, blocks, faces,
):
    def degree(k, carry):
        x = jnp.concatenate([derivs[k, q] for q in range(NQ)], axis=1)
        blocks[...] = matmul(stiff_ref[...], stacked(x, LANES))

        def finish(p, rows, total):
            derivs[k + 1, p, rows, :] = total

        contract_star(blocks, 0, star_ref, finish)
        return carry

    for k in range(DERIVS - 1):
        degree(k, 0)
    if tick == 0:
        now = [STEP ** (k + 1) / FACTORIALS[k] for k in range(DERIVS)]
    else:
        now = tick_weights(period_ref[0:1, :], tick)
    parts = []
    for q in range(NQ):
        parts.append(weighted(derivs, q, now))
    faces[...] = matmul(proj_ref[...], stacked(jnp.concatenate(parts, axis=1), LANES))
    highs, lows = [], []
    for q in range(NQ):
        row = jnp.concatenate(
            [
                faces[f * FACE_ROWS : (f + 1) * FACE_ROWS, q * LANES : (q + 1) * LANES]
                for f in range(FACES)
            ],
            axis=1,
        )
        high, low = split_pair(row)
        table_ref[q * FACE_ROWS : (q + 1) * FACE_ROWS, :] = high
        table_ref[TABLE + q * FACE_ROWS : TABLE + (q + 1) * FACE_ROWS, :] = low
    both = matmul(table_ref[...], send_ref[...])
    picked = both[:TABLE] + both[TABLE:]
    near_list_ref[...] = picked[:, :LANES]
    far_list_ref[...] = picked[:, LANES:]


def begin_kernel(
    coef_ref, star_ref, stiffness_ref, projection_ref, faces_ref,
    derivs, table_ref, near_list_ref, far_list_ref,
    stiff_ref, proj_ref, send_ref,
    blocks, faces, work,
):
    derivs[0] = jnp.zeros((NQ, ROWS, LANES), F32)
    for q in range(NQ):
        derivs[0, q, 0:BASIS, :] = coef_ref[q]
    work[...] = jnp.zeros_like(work)
    for d in range(3):
        weights_into(work, d * ROWS, -stiffness_ref[d], ROWS)
    stiff_ref[...] = work[0 : 3 * ROWS, :].astype(BF16)
    work[...] = jnp.zeros_like(work)
    for f in range(FACES):
        weights_into(work, f * FACE_ROWS, projection_ref[:, f, :], ROWS)
    proj_ref[...] = work[0 : FACES * FACE_ROWS, :].astype(BF16)
    column = lax.broadcasted_iota(jnp.int32, (FACES * LANES, LANES), 0)
    near = jnp.concatenate([faces_ref[3:4, :], faces_ref[0:1, :]], axis=1)
    far = jnp.concatenate([faces_ref[1:2, :], faces_ref[2:3, :]], axis=1)
    send_ref[:, :LANES] = (column == near).astype(F32).astype(BF16)
    send_ref[:, LANES:] = (column == far).astype(F32).astype(BF16)
    predict_and_send(
        0, star_ref, stiff_ref, proj_ref, send_ref, None,
        derivs, table_ref, near_list_ref, far_list_ref, blocks, faces,
    )


def relay_kernel(gathered_ref, far_list_ref, first_ref, second_ref):
    me = lax.axis_index("region")
    other = 1 - lax.rem(me, 2)
    even = lax.rem(me // 2, 2) == 0
    lane = lax.broadcasted_iota(jnp.int32, (TABLE, LANES), 1)
    partner = gathered_ref[other]
    own = far_list_ref[...]
    upward = jnp.where(lane < LANES // 2, partner, own)
    downward = jnp.where(lane < LANES // 2, own, partner)
    first_ref[...] = jnp.where(even, downward, upward)
    second_ref[...] = jnp.where(even, upward, downward)


def face_contract(source, solver_ref, side, into):
    for f in range(FACES):
        totals = [None] * NQ
        for q in range(NQ):
            block = source(q, f)
            for p in range(NQ):
                term = block * solver_ref[side, f, q, p : p + 1, :]
                totals[p] = term if totals[p] is None else totals[p] + term
        for p in range(NQ):
            into[f * FACE_ROWS : (f + 1) * FACE_ROWS, p * LANES : (p + 1) * LANES] = totals[p]


def ending_mask(period, tick):
    return period <= ((tick + 1) & -(tick + 1))


def own_body(
    tick, derivs, table_ref, sum_ref, star_ref, solver_ref, period_ref,
    both_ref, lift_ref, local_ref, base_ref, partial_ref, big, flux,
):
    period = period_ref[0:1, :]
    ending = ending_mask(period, tick)
    whole = own_weights(period)
    own = jnp.concatenate([weighted(derivs, q, whole) for q in range(NQ)], axis=1)
    big[...] = matmul(both_ref[...], stacked(own, LANES))
    face_contract(
        lambda q, f: big[f * FACE_ROWS : (f + 1) * FACE_ROWS, q * LANES : (q + 1) * LANES],
        solver_ref, 0, flux,
    )
    lifted = matmul(lift_ref[...], stacked(flux[...], 192))
    for p in range(NQ):
        base_ref[p] = lifted[:, p * LANES : (p + 1) * LANES]

    def finish(p, rows, total):
        change = total - base_ref[p, rows, :]
        base_ref[p, rows, :] = derivs[0, p, rows, :] + jnp.where(ending, change, 0.0)

    contract_star(big, FACES * FACE_ROWS, star_ref, finish)
    both = matmul(table_ref[...], local_ref[...])
    picked = both[:TABLE] + both[TABLE:]
    if sum_ref is None:
        partial_ref[...] = picked
    else:
        cleared = ending_mask(period, tick - 1)
        for f in range(FACES):
            where = slice(f * LANES, (f + 1) * LANES)
            partial_ref[:, where] = picked[:, where] + jnp.where(cleared, 0.0, sum_ref[:, where])


def own_first_kernel(
    derivs, table_ref, star_ref, solver_ref, cluster_ref,
    stiffness_ref, projection_ref, lifting_ref, neighbor_ref, order_ref,
    base_ref, partial_ref, both_ref, lift_ref, local_ref, remote_ref, period_ref,
    big, flux, work, work_lift,
):
    lane = lax.broadcasted_iota(jnp.int32, (8, LANES), 1)
    period = jnp.full((8, LANES), 1, jnp.int32)
    for j in range(LANES // 16):
        c = cluster_ref[j]
        p = jnp.where(c == 0, 1, jnp.where(c == 1, 2, 4))
        period = jnp.where((lane >> 4) == j, p, period)
    period_ref[...] = period
    work[...] = jnp.zeros_like(work)
    for f in range(FACES):
        weights_into(work, f * FACE_ROWS, projection_ref[:, f, :], ROWS)
    for d in range(3):
        weights_into(work, FACES * FACE_ROWS + d * ROWS, stiffness_ref[d].T, ROWS)
    both_ref[...] = work[...].astype(BF16)
    work_lift[...] = jnp.zeros_like(work_lift)
    lifts = jnp.zeros((BASIS, 192), F32)
    for f in range(FACES):
        high, low = split_pair(lifting_ref[f])
        for part, offset in ((high, 0), (high, 64), (low, 128)):
            lifts = lifts + placed(part, offset + f * FACE_ROWS, 192, 0)
    work_lift[0:BASIS, :] = lifts
    lift_ref[...] = work_lift[...].astype(BF16)
    column = lax.broadcasted_iota(jnp.int32, (LANES, LANES), 0)
    for f in range(FACES):
        row = neighbor_ref[f : f + 1, :]
        for g in range(6):
            chosen = (column + g * LANES == row).astype(F32).astype(BF16)
            if g < FACES:
                local_ref[g * LANES : (g + 1) * LANES, f * LANES : (f + 1) * LANES] = chosen
            else:
                start = (g - FACES) * LANES
                remote_ref[start : start + LANES, f * LANES : (f + 1) * LANES] = chosen
    own_body(
        0, derivs, table_ref, None, star_ref, solver_ref, period_ref,
        both_ref, lift_ref, local_ref, base_ref, partial_ref, big, flux,
    )


def own_kernel(
    tick, derivs, table_ref, sum_ref, star_ref, solver_ref, period_ref,
    both_ref, lift_ref, local_ref, order_ref,
    base_ref, partial_ref, big, flux,
):
    own_body(
        tick, derivs, table_ref, sum_ref, star_ref, solver_ref, period_ref,
        both_ref, lift_ref, local_ref, base_ref, partial_ref, big, flux,
    )


def near_body(
    tick, first_ref, second_ref, gathered_ref, base_ref, partial_ref, solver_ref, period_ref,
    lift_ref, remote_ref, sums, flux,
):
    me = lax.axis_index("region")
    core = lax.rem(me, 2)
    even = lax.rem(me // 2, 2) == 0
    lane = lax.broadcasted_iota(jnp.int32, (TABLE, LANES), 1)
    low_half = lane < LANES // 2
    partner = gathered_ref[1 - core]
    first, second = first_ref[...], second_ref[...]
    upward = jnp.where(even, first, second)
    downward = jnp.where(even, second, first)
    lower = jnp.where(jnp.logical_and(core == 1, low_half), partner, upward)
    upper = jnp.where(
        jnp.logical_and(core == 0, jnp.logical_not(low_half)), partner, downward
    )
    high, low = split_pair(jnp.concatenate([lower, upper], axis=1))
    both = matmul(jnp.concatenate([high, low], axis=0), remote_ref[...])
    sums[...] = partial_ref[...] + both[:TABLE] + both[TABLE:]
    face_contract(
        lambda q, f: sums[q * FACE_ROWS : (q + 1) * FACE_ROWS, f * LANES : (f + 1) * LANES],
        solver_ref, 1, flux,
    )
    return matmul(lift_ref[...], stacked(flux[...], 192))


def step_kernel(
    tick, first_ref, second_ref, gathered_ref, base_ref, partial_ref, star_ref, solver_ref,
    period_ref, lift_ref, remote_ref, stiff_ref, proj_ref, send_ref,
    derivs, sums, table_ref, near_list_ref, far_list_ref,
    flux, blocks, faces,
):
    lifted = near_body(
        tick, first_ref, second_ref, gathered_ref, base_ref, partial_ref, solver_ref, period_ref,
        lift_ref, remote_ref, sums, flux,
    )
    ending = ending_mask(period_ref[0:1, :], tick)
    for p in range(NQ):
        change = jnp.where(ending, lifted[:, p * LANES : (p + 1) * LANES], 0.0)
        value = base_ref[p] - change
        derivs[0, p] = value
    predict_and_send(
        tick + 1, star_ref, stiff_ref, proj_ref, send_ref, period_ref,
        derivs, table_ref, near_list_ref, far_list_ref, blocks, faces,
    )


def end_kernel(
    first_ref, second_ref, gathered_ref, base_ref, partial_ref, solver_ref,
    period_ref, lift_ref, remote_ref,
    out_ref, sums, flux,
):
    tick = TICKS - 1
    lifted = near_body(
        tick, first_ref, second_ref, gathered_ref, base_ref, partial_ref, solver_ref, period_ref,
        lift_ref, remote_ref, sums, flux,
    )
    for p in range(NQ):
        out_ref[p] = (base_ref[p] - lifted[:, p * LANES : (p + 1) * LANES])[0:BASIS, :]


VMEM = pl.BlockSpec(memory_space=pltpu.VMEM)
SMEM = pl.BlockSpec(memory_space=pltpu.SMEM)


def call(kernel, name, inputs, outputs, scratch, flops, in_specs=None):
    return pl.pallas_call(
        kernel,
        name=name,
        out_shape=[jax.ShapeDtypeStruct(s, d) for s, d in outputs],
        in_specs=in_specs or [VMEM] * len(inputs),
        out_specs=[VMEM] * len(outputs),
        scratch_shapes=[pltpu.VMEM(s, d) for s, d in scratch],
        cost_estimate=pl.CostEstimate(flops=flops, bytes_accessed=flops // 100, transcendentals=0),
        compiler_params=pltpu.CompilerParams(vmem_limit_bytes=24 << 20),
    )(*inputs)


STATE = ((NQ, ROWS, LANES), F32)
PAIRED = ((2 * TABLE, FACES * LANES), BF16)
SUMS = ((TABLE, FACES * LANES), F32)
LIST = ((TABLE, LANES), F32)
DERIV = ((DERIVS, NQ, ROWS, LANES), F32)
BLOCKS = ((3 * ROWS, WIDE), F32)
FACE = ((FACES * FACE_ROWS, WIDE), F32)
BOTH_ROWS = FACES * FACE_ROWS + 3 * ROWS
BIG = ((BOTH_ROWS, WIDE), F32)


def per_device(
    coefficients, star, solvers, stiffness, projection, lifting, block_cluster, neighbors, send_faces
):
    projection = jnp.transpose(projection, (1, 0, 2))
    count = lax.axis_size("region")
    cores = [[2 * k, 2 * k + 1] for k in range(count // 2)]
    pairs = ([], [])
    for i in range(count - 2):
        pairs[(i // 2) % 2] .extend([(i, i + 2), (i + 2, i)])
    inner, outer = pairs

    (derivs, table, near_list, far_list, stiff_w, proj_w, send_w) = call(
        begin_kernel, "begin",
        (coefficients, star, stiffness, projection, send_faces),
        (
            DERIV, PAIRED, LIST, LIST,
            ((3 * ROWS, LANES), BF16), ((FACES * FACE_ROWS, LANES), BF16),
            ((FACES * LANES, 2 * LANES), BF16),
        ),
        (BLOCKS, FACE, ((3 * ROWS, LANES), F32)),
        10**9,
    )
    sums = None
    for tick in range(TICKS):
        gathered = lax.all_gather(near_list, "region", axis_index_groups=cores)
        first, second = call(
            relay_kernel, "relay", (gathered, far_list), (LIST, LIST), (), 10**6
        )
        first_in = lax.ppermute(first, "region", outer)
        second_in = lax.ppermute(second, "region", inner)
        if tick == 0:
            base, partial, both_w, lift_w, local_w, remote_w, period = call(
                own_first_kernel, "own_first",
                (
                    derivs, table, star, solvers, block_cluster,
                    stiffness, projection, lifting, neighbors, first[:8],
                ),
                (
                    STATE, SUMS, ((BOTH_ROWS, LANES), BF16), ((ROWS, 192), BF16),
                    ((FACES * LANES, FACES * LANES), BF16), ((2 * LANES, FACES * LANES), BF16),
                    ((8, LANES), jnp.int32),
                ),
                (BIG, FACE, ((BOTH_ROWS, LANES), F32), ((ROWS, 192), F32)),
                10**9,
                [VMEM] * 4 + [SMEM] + [VMEM] * 5,
            )
        else:
            base, partial = call(
                functools.partial(own_kernel, tick), "own",
                (derivs, table, sums, star, solvers, period, both_w, lift_w, local_w, first[:8]),
                (STATE, SUMS), (BIG, FACE), 10**9,
            )
        if tick < TICKS - 1:
            derivs, sums, table, near_list, far_list = call(
                functools.partial(step_kernel, tick), "step",
                (
                    first_in, second_in, gathered, base, partial, star, solvers,
                    period, lift_w, remote_w, stiff_w, proj_w, send_w,
                ),
                (DERIV, SUMS, PAIRED, LIST, LIST),
                (FACE, BLOCKS, FACE), 10**9,
            )
    (updated,) = call(
        end_kernel, "end",
        (first_in, second_in, gathered, base, partial, solvers, period, lift_w, remote_w),
        (((NQ, BASIS, LANES), F32),), (SUMS, FACE), 10**9,
    )
    return updated


def solution(mesh):
    placed_specs = (
        P(None, None, "region"),
        P(None, None, None, "region"),
        P(None, None, None, None, "region"),
        P(),
        P(),
        P(),
        P("region"),
        P(None, "region"),
        P(None, "region"),
    )
    return jax.shard_map(
        per_device, mesh=mesh, in_specs=placed_specs, out_specs=P(None, None, "region"),
        check_vma=False,
    )
```
